32 devices in a mesh: dp: 4 (over x, core), expert: 8 (over z, y).
Axes of the slice: x: 2, y: 2, z: 4, core: 2. Of those that a mesh axis runs over, the one named last changes fastest.
Arguments:
- tokens: bfloat16 [4096, 4096], P(('dp', 'expert')), may hold values from -6 to 6
- router: bfloat16 [4096, 8], replicated, may hold values from -0.09375 to 0.09375
- price: float32 [8], replicated, may hold values from -1 to 1
- w_in: bfloat16 [8, 4096, 8192], P('expert', None, 'dp'), may hold values from -0.09375 to 0.09375
- w_out: bfloat16 [8, 8192, 4096], P('expert', 'dp'), may hold values from -0.0625 to 0.0625
- assign: int32 [4096], P(('dp', 'expert')), may hold values from 0 to 7, as said below
Outputs:
- mixed: bfloat16 [4096, 4096], P(('dp', 'expert'))
- new_price: float32 [8], replicated
The draws below stay inside these ranges and needn't reach their ends.
Inputs may be any that keep to these rules, and one draw needn't show every extreme that they name: `assign`: every expert is named by exactly 512 tokens in all, and by at most 24 of the 128 tokens of one device (aligned blocks of 128 rows); on every device some expert is named exactly 24 times, and the experts' loads on one device are, in some order, the same 8 numbers on every device.
All inputs are finite; a program needn't handle non-finite values.
Results may differ from the reference program's by a relative error of at most 0.013.
Values may be sent and summed in bfloat16 or wider, within the bound.
A program may use at most 128 MiB of HBM per device.

```python
import jax
import jax.numpy as jnp
from jax import lax

D = 4096
FFW = 8192
TOK_DEV = 128
EXPERTS = 8
TOKENS = 4096
FF_DEV = 2048


def expert_labels(key):
    blocks = TOKENS // TOK_DEV
    half = EXPERTS // 2
    mean_load = TOK_DEV // EXPERTS
    which = jnp.arange(EXPERTS, dtype=jnp.int32)
    mirror = jnp.minimum(which, EXPERTS - 1 - which)
    lift = mean_load // 2 * (half - mirror) // half
    base = jnp.where(which < half, mean_load + lift, mean_load - lift).astype(jnp.int32)
    group_count = blocks // EXPERTS
    group_keys = jax.random.split(jax.random.fold_in(key, 11), group_count)
    perms = jax.vmap(lambda sub: jax.random.permutation(sub, EXPERTS))(group_keys).astype(jnp.int32)
    block_ids = jnp.arange(blocks, dtype=jnp.int32)
    shifts = perms[block_ids // EXPERTS]
    counts = base[(shifts + block_ids[:, None]) % EXPERTS]

    def one_block(count_row, sub):
        labels = jnp.repeat(jnp.arange(EXPERTS, dtype=jnp.int32), count_row, total_repeat_length=TOK_DEV)
        return jax.random.permutation(sub, labels)
    block_keys = jax.random.split(jax.random.fold_in(key, 23), blocks)
    return jax.vmap(one_block)(counts, block_keys).astype(jnp.int32)


def draw_assign(key, part):
    return expert_labels(key).reshape(TOKENS)


def level_of(key, dims, shards, smallest, largest):
    factor_of = 1.0
    for position, shards_of in shards:
        draws = jax.random.uniform(jax.random.fold_in(jax.random.fold_in(key, 6), position), (shards_of,), jnp.float32, smallest / len(shards), largest / len(shards))
        factor_of = factor_of * jnp.repeat(jnp.exp(draws), dims[position] // shards_of).reshape((-1,) + (1,) * (len(dims) - 1 - position))
    return factor_of


def gaussian(stream_key, dims, deviation, reach, cuts=(), held_as=jnp.bfloat16):
    level = level_of(stream_key, dims, cuts, -0.22, 0.18) if cuts else 1.0
    drawn = jax.random.normal(stream_key, dims, jnp.float32) * deviation * level
    return jnp.minimum(jnp.maximum(drawn, -reach), reach).astype(held_as)


def setup_inputs(seed: int = 0) -> dict:
    arg_keys = jax.random.split(jax.random.key(seed), 7)
    return {
        "tokens": gaussian(arg_keys[0], (TOKENS, D), 1.0, 6.0, ((0, 32),)),
        "router": gaussian(arg_keys[1], (D, EXPERTS), D ** -0.5, 0.09375),
        "price": jnp.clip(jax.random.uniform(arg_keys[2], (EXPERTS,), jnp.float32, -1.0, 1.0), -1.0, 1.0),
        "w_in": gaussian(arg_keys[3], (EXPERTS, D, FFW), D ** -0.5, 0.09375, ((0, 8), (2, 4))),
        "w_out": gaussian(arg_keys[4], (EXPERTS, FFW, D), FFW ** -0.5, 0.0625, ((0, 8), (1, 4))),
        "assign": draw_assign(jax.random.fold_in(arg_keys[6], 71), 0),
    }


BID_STEP = 0.01


def reference(tokens, router, price, w_in, w_out, assign):
    affinity = jnp.dot(tokens, router, preferred_element_type=jnp.float32)
    onehot = assign[:, None] == jnp.arange(EXPERTS, dtype=jnp.int32)[None, :]
    own = jnp.sum(jnp.where(onehot, affinity, 0.0), axis=1)
    rival = jnp.max(jnp.where(onehot, -1e30, affinity - price[None, :]), axis=1)
    bid = own - rival + BID_STEP
    new_price = jnp.max(jnp.where(onehot, bid[:, None], -1e30), axis=0)
    per_expert = TOKENS // EXPERTS
    order = jnp.argsort(assign, stable=True).astype(jnp.int32)
    groups = order.reshape(EXPERTS, per_expert)

    def run_expert(packed):
        index, first, second = packed
        rows = tokens[index].astype(jnp.float32)
        hidden = jax.nn.gelu(jnp.dot(rows, first.astype(jnp.float32)), approximate=True).astype(jnp.bfloat16)
        total = jnp.zeros((per_expert, D), jnp.float32)
        for block in range(FFW // FF_DEV):
            low = block * FF_DEV
            part = jnp.dot(hidden[:, low:low + FF_DEV].astype(jnp.float32), second[low:low + FF_DEV].astype(jnp.float32))
            part = lax.optimization_barrier(part.astype(jnp.bfloat16))
            total = total + part.astype(jnp.float32)
        return total.astype(jnp.bfloat16)

    outputs = lax.map(run_expert, (groups, w_in, w_out))
    expert_out = jnp.zeros((TOKENS, D), outputs.dtype).at[groups.reshape(-1)].set(outputs.reshape(-1, D))
    gate = jax.nn.sigmoid(own)
    mixed = (gate[:, None] * expert_out.astype(jnp.float32)).astype(jnp.bfloat16)
    return mixed, new_price
```

```python
import functools

import jax
import jax.numpy as jnp
from jax import lax
from jax.experimental import pallas as pl
from jax.experimental.pallas import tpu as pltpu
from jax.sharding import PartitionSpec as P

BID_STEP = 0.01
EARLY = 7
MESH = pl.DeviceIdType.MESH
SCHED = (
    "s6", "s2", "s3", "s1", "s7", "s4", "s5", "a1", "a0", "a3", "w0", "w1",
    "b0", "c0", "a2", "f0", "g0", "w3", "w2", "a7", "a6", "b1", "c1", "f1",
    "a5", "g1", "w6", "a4", "w7", "p3", "b3", "c3", "f3", "w5", "g3", "h0",
    "p7", "w4", "p6", "b2", "r7", "p2", "c2", "f2", "p1", "r6", "r3", "g2",
    "p4", "r4", "p5", "p0", "r2", "r1", "r5", "r0",
)


def schedule(groups):
    if groups == 4:
        return SCHED
    order = [0] + list(range(groups - 1, 0, -1))
    steps = []
    for g in order[1:]:
        steps += [("s", 2 * g), ("s", 2 * g + 1)]
    steps += [("s", 1), ("a", 0), ("a", 1), ("w", 0), ("w", 1)]
    for i, g in enumerate(order):
        after = order[i + 1] if i + 1 < groups else None
        before = order[i - 1] if i else None
        steps += [("b", g)]
        if after is not None:
            steps += [("a", 2 * after)]
        steps += [("c", g), ("f", g)]
        if after is not None:
            steps += [("a", 2 * after + 1)]
        steps += [("g", g)]
        if after is not None:
            steps += [("w", 2 * after), ("w", 2 * after + 1)]
        steps += [("p", 2 * g), ("p", 2 * g + 1)]
        if before is not None:
            steps += [("r", 2 * before), ("r", 2 * before + 1)]
        if i == 1:
            steps += [("h", 0)]
    g = order[-1]
    steps += [("r", 2 * g), ("r", 2 * g + 1)]
    return [name + str(k) for name, k in steps]


def remote(src, dst, send, recv, a, b):
    return pltpu.make_async_remote_copy(
        src_ref=src, dst_ref=dst, send_sem=send, recv_sem=recv, device_id=(a, b), device_id_type=MESH
    )


def signal(dps, experts, a, b):
    barrier = pltpu.get_barrier_semaphore()
    for k in range(1, experts):
        pl.semaphore_signal(barrier, inc=1, device_id=(a, lax.rem(b + k, experts)), device_id_type=MESH)
    for k in range(1, dps):
        pl.semaphore_signal(barrier, inc=1, device_id=(lax.rem(a + k, dps), b), device_id_type=MESH)


def meet(dps, experts):
    pl.semaphore_wait(pltpu.get_barrier_semaphore(), experts + dps - 2)


def layer_kernel(
    dps, experts, capacity, spill, assign, price, router, tokens, w_in, w_out, back, pick, gate, prices, *refs
):
    if spill:
        rows, refs = refs[0], refs[1:]
        loaded, refs = refs[0], refs[1:]
    else:
        rows, refs = refs[0], refs[1:]
        loaded = None
    packed, best, bests, all_bests, win, wout, flat, hidden, part, pair, far, final, top = refs[:13]
    load_sem, own_sem, s1, r1, s2, r2, s3, r3, s4, r4, s5, r5, s6, r6, sb, rb, sd, rd = refs[13:]
    a, b = lax.axis_index("dp"), lax.axis_index("expert")
    nx, groups = dps // 2, experts // 2
    x, c = a // 2, lax.rem(a, 2)
    z, y = b // 2, lax.rem(b, 2)
    other = 2 * x + 1 - c
    count, width = tokens.shape
    ff = win.shape[1]
    cut = 512
    wide = 1024
    tall = 2 * dps * capacity
    load_in = pltpu.make_async_copy(w_in, win, load_sem.at[0])
    load_out = pltpu.make_async_copy(w_out, wout, load_sem.at[1])
    load_in.start()
    load_out.start()
    signal(dps, experts, a, b)

    order = list(range(groups))

    def behind(k):
        to = z
        for bit in range(groups.bit_length()):
            if order[k // 2] >> bit & 1:
                to = to + (1 - 2 * lax.rem(z // 2**bit, 2)) * 2**bit
        return 2 * to + lax.rem(y + k % 2, 2)

    ahead = behind

    def xrow(q):
        return 2 * lax.rem(x + q, nx) + c

    def xback(q):
        return 2 * lax.rem(x + nx - q, nx) + c

    def out(k):
        e = ahead(k)
        return remote(packed.at[k], rows.at[k, a], s1.at[k], r1.at[k], a, e)

    def out_best(k):
        return remote(best, bests.at[k], sb.at[k], rb.at[k], a, ahead(k))

    def spread_best(k):
        return remote(top, all_bests.at[k], sd.at[k], rd.at[k], lax.rem(a + k, dps), b)

    def fan(q, k):
        return remote(rows.at[k, a], rows.at[k, a], s2.at[q - 1, k], r2.at[q - 1, k], xrow(q), b)

    def fan_in(q, k):
        row = xback(q)
        return remote(rows.at[k, row], rows.at[k, row], s2.at[q - 1, k], r2.at[q - 1, k], row, b)

    def share(q, k):
        row = xback(q)
        return remote(rows.at[k, row], rows.at[k, row], s3.at[q, k], r3.at[q, k], other, b)

    def share_in(q, k):
        row = xback(q) + 1 - 2 * c
        return remote(rows.at[k, row], rows.at[k, row], s3.at[q, k], r3.at[q, k], other, b)

    def beside(q, k):
        return remote(
            part.at[k, xrow(q) + 1 - 2 * c], pair.at[q, k], s4.at[q, k], r4.at[q, k], other, b
        )

    def across(q, k):
        return remote(pair.at[q, k], far.at[q - 1, k], s5.at[q - 1, k], r5.at[q - 1, k], xrow(q), b)

    def home(k):
        return remote(final.at[k], back.at[b], s6.at[k], r6.at[k], a, behind(k))

    own = pltpu.make_async_copy(packed.at[0], rows.at[0, a], own_sem.at[0])
    own_back = pltpu.make_async_copy(final.at[0], back.at[b], own_sem.at[2])

    def arrive(k):
        if k == 0:
            own.wait()
        else:
            out(k).wait_recv()
        for q in range(1, nx):
            fan(q, k).start()
        share(0, k).start()

    def forward(k):
        for q in range(1, nx):
            fan_in(q, k).wait_recv()
            share(q, k).start()

    def first(t, carry):
        cols = pl.ds(pl.multiple_of(t * wide, wide), wide)
        raw = jnp.dot(flat[...], win[:, cols], preferred_element_type=jnp.float32)
        hidden[:, cols] = jax.nn.gelu(raw, approximate=True).astype(jnp.bfloat16)
        return carry

    def begin(g):
        for k in (2 * g, 2 * g + 1):
            for q in range(nx):
                share_in(q, k).wait_recv()
        if spill:
            load = pltpu.make_async_copy(rows.at[pl.ds(2 * g, 2)], loaded, own_sem.at[1])
            load.start()
            load.wait()

        def flatten(t, carry):
            cols = pl.ds(pl.multiple_of(t * cut, cut), cut)
            source = loaded[:, :, :, cols] if spill else rows[2 * g : 2 * g + 2, :, :, cols]
            block = source.astype(jnp.float32)
            flat[:, cols] = block.reshape(tall, cut).astype(jnp.bfloat16)
            return carry

        lax.fori_loop(0, width // cut, flatten, 0)
        if not waited:
            load_in.wait()
        lax.fori_loop(0, ff // wide // 2, first, 0)

    def middle(g):
        lax.fori_loop(ff // wide // 2, ff // wide, first, 0)
        if not waited:
            load_out.wait()
            waited.append(g)

    def finish(g, half):
        def second(t, carry):
            cols = pl.ds(pl.multiple_of(t * wide, wide), wide)
            res = jnp.dot(hidden[...], wout[:, cols], preferred_element_type=jnp.float32)
            part[2 * g : 2 * g + 2, :, :, cols] = res.reshape(2, dps, capacity, wide).astype(jnp.bfloat16)
            return carry

        steps = width // wide
        lax.fori_loop(half * steps // 2, (half + 1) * steps // 2, second, 0)
        if half == 1:
            for k in (2 * g, 2 * g + 1):
                for q in list(range(1, nx)) + [0]:
                    beside(q, k).start()

    def add_pair(k):
        if True:
            for q in range(1, nx):
                beside(q, k).wait_recv()

                def add(t, carry):
                    cols = pl.ds(pl.multiple_of(t * cut, cut), cut)
                    total = part[k, xrow(q), :, cols].astype(jnp.float32)
                    total = total + pair[q, k, :, cols].astype(jnp.float32)
                    pair[q, k, :, cols] = total.astype(jnp.bfloat16)
                    return carry

                lax.fori_loop(0, width // cut, add, 0)
                across(q, k).start()

    def add_far(k):
        if True:
            beside(0, k).wait_recv()
            for q in range(1, nx):
                across(q, k).wait_recv()

            def add(t, carry):
                cols = pl.ds(pl.multiple_of(t * cut, cut), cut)
                total = part[k, a, :, cols].astype(jnp.float32)
                total = total + pair[0, k, :, cols].astype(jnp.float32)
                for q in range(1, nx):
                    total = total + far[q - 1, k, :, cols].astype(jnp.float32)
                final[k, :, cols] = total.astype(jnp.bfloat16)
                return carry

            lax.fori_loop(0, width // cut, add, 0)
            if k == 0:
                own_back.start()
            else:
                home(k).start()

    def highest_bid():
        for k in range(1, experts):
            out_best(k).wait_recv()
        highest = best[...]
        for k in range(1, experts):
            highest = jnp.maximum(highest, bests[k])
        top[...] = highest
        all_bests[0] = highest
        for k in range(1, dps):
            spread_best(k).start()

    waited = []
    named = assign[...]
    upper = lax.broadcasted_iota(jnp.int32, (count, count), 0)
    lower = lax.broadcasted_iota(jnp.int32, (count, count), 1)
    onehot = lax.broadcasted_iota(jnp.int32, (experts, count), 0) == named
    before = jnp.where(upper <= lower, 1.0, 0.0).astype(jnp.bfloat16)
    running = jnp.dot(
        jnp.where(onehot, 1.0, 0.0).astype(jnp.bfloat16), before, preferred_element_type=jnp.float32
    )
    slot = jnp.sum(jnp.where(onehot, running, 0.0), axis=0, keepdims=True).astype(jnp.int32) - 1
    place = named * capacity + slot

    def pack(low, high):
        lines = lax.broadcasted_iota(jnp.int32, (capacity, count), 0)
        chosen = jnp.concatenate(
            [jnp.where(place == ahead(k) * capacity + lines, 1.0, 0.0) for k in range(low, high)], axis=0
        ).astype(jnp.bfloat16)

        def some(t, carry):
            cols = pl.ds(pl.multiple_of(t * cut, cut), cut)
            block = jnp.dot(chosen, tokens[:, cols], preferred_element_type=jnp.float32)
            packed[low:high, :, cols] = block.reshape(high - low, capacity, cut).astype(jnp.bfloat16)
            return carry

        lax.fori_loop(0, width // cut, some, 0)

    def bids():
        affinity = lax.dot_general(
            router[...], tokens[...], (((1,), (1,)), ((), ())), preferred_element_type=jnp.float32
        )
        corner = lax.broadcasted_iota(jnp.int32, (experts, experts), 0) == lax.broadcasted_iota(
            jnp.int32, (experts, experts), 1
        )
        cost = jnp.sum(jnp.where(corner, price[...], 0.0), axis=1, keepdims=True)
        mine = jnp.sum(jnp.where(onehot, affinity, 0.0), axis=0, keepdims=True)
        rival = jnp.max(jnp.where(onehot, -1e30, affinity - cost), axis=0, keepdims=True)
        bid = mine - rival + BID_STEP
        high = jnp.max(jnp.where(onehot, bid, -1e30), axis=1, keepdims=True)
        best[...] = jnp.broadcast_to(high, best.shape)
        gate[...] = jax.nn.sigmoid(mine)
        diagonal = upper == lower
        spot = jnp.sum(jnp.where(diagonal, place.astype(jnp.float32), 0.0), axis=1, keepdims=True)
        slots = lax.broadcasted_iota(jnp.int32, (count, experts * capacity), 1)
        pick[...] = jnp.where(spot.astype(jnp.int32) == slots, 1.0, 0.0).astype(jnp.bfloat16)

    pack(0, experts)
    meet(dps, experts)
    own.start()
    early = [op for op in schedule(groups) if op[0] == "s"]
    for op in early[: EARLY]:
        out(int(op[1:])).start()
    bids()
    for k in range(1, experts):
        out_best(k).start()
    table = dict(s=lambda k: out(k).start(), a=arrive, w=forward, b=begin, c=middle, f=lambda g: finish(g, 0), g=lambda g: finish(g, 1), p=add_pair, r=add_far, h=lambda k: highest_bid())
    for op in schedule(groups):
        if op in early[:EARLY]:
            continue
        table[op[0]](int(op[1:]))
    own_back.wait()
    total = all_bests[0]
    for k in range(1, dps):
        spread_best(k).wait_recv()
        total = jnp.maximum(total, all_bests[k])
    square = (experts, experts)
    corner = lax.broadcasted_iota(jnp.int32, square, 0) == lax.broadcasted_iota(jnp.int32, square, 1)
    prices[...] = jnp.max(jnp.where(corner, total[:, :experts], -1e30), axis=0, keepdims=True)
    for k in range(1, dps):
        spread_best(k).wait_send()
    for k in range(1, experts):
        e = ahead(k)
        remote(final.at[k], back.at[e], s6.at[k], r6.at[k], a, e).wait_recv()
        home(k).wait_send()
        out(k).wait_send()
        out_best(k).wait_send()
    for k in range(experts):
        for q in range(1, nx):
            fan(q, k).wait_send()
            across(q, k).wait_send()
        for q in range(nx):
            share(q, k).wait_send()
            beside(q, k).wait_send()


def layer(assign, price, router, tokens, w_in, w_out, dps, capacity):
    experts = router.shape[0]
    count, width = tokens.shape
    nx = dps // 2
    ff = w_in.shape[1]
    tall = 2 * dps * capacity
    dtype = tokens.dtype
    sem = pltpu.SemaphoreType.DMA
    anywhere = pl.BlockSpec(memory_space=pl.ANY)
    inside = pl.BlockSpec(memory_space=pltpu.VMEM)
    landing = (experts, dps, capacity, width)
    note = (experts, 128)
    spill = experts * dps * capacity * width > 4 * 1024 * 1024
    outs = [
        jax.ShapeDtypeStruct((experts, capacity, width), dtype),
        jax.ShapeDtypeStruct((count, experts * capacity), jnp.bfloat16),
        jax.ShapeDtypeStruct((1, count), jnp.float32),
        jax.ShapeDtypeStruct((1, experts), jnp.float32),
    ]
    places = [anywhere, inside, inside, inside]
    if spill:
        outs.append(jax.ShapeDtypeStruct(landing, dtype))
        places.append(anywhere)
        held = [pltpu.VMEM((2, dps, capacity, width), dtype)]
    else:
        held = [pltpu.VMEM(landing, dtype)]
    return pl.pallas_call(
        functools.partial(layer_kernel, dps, experts, capacity, spill),
        out_shape=tuple(outs),
        in_specs=[inside, inside, inside, inside, anywhere, anywhere],
        out_specs=tuple(places),
        scratch_shapes=held + [
            pltpu.VMEM((experts, capacity, width), dtype),
            pltpu.VMEM(note, jnp.float32),
            pltpu.VMEM((experts,) + note, jnp.float32),
            pltpu.VMEM((dps,) + note, jnp.float32),
            pltpu.VMEM((width, ff), dtype),
            pltpu.VMEM((ff, width), dtype),
            pltpu.VMEM((tall, width), dtype),
            pltpu.VMEM((tall, ff), dtype),
            pltpu.VMEM((experts, dps, capacity, width), dtype),
            pltpu.VMEM((nx, experts, capacity, width), dtype),
            pltpu.VMEM((nx - 1, experts, capacity, width), dtype),
            pltpu.VMEM((experts, capacity, width), dtype),
            pltpu.VMEM(note, jnp.float32),
            sem((2,)),
            sem((3,)),
            sem((experts,)),
            sem((experts,)),
            sem((nx - 1, experts)),
            sem((nx - 1, experts)),
            sem((nx, experts)),
            sem((nx, experts)),
            sem((nx, experts)),
            sem((nx, experts)),
            sem((nx - 1, experts)),
            sem((nx - 1, experts)),
            sem((experts,)),
            sem((experts,)),
            sem((experts,)),
            sem((experts,)),
            sem((dps,)),
            sem((dps,)),
        ],
        compiler_params=pltpu.CompilerParams(
            collective_id=0, has_side_effects=True, vmem_limit_bytes=63 * 1024 * 1024
        ),
        name="layer",
    )(assign, price, router, tokens, w_in, w_out)


def shards(tokens, router, price, w_in, w_out, assign):
    experts = router.shape[1]
    count, width = tokens.shape
    capacity = -(-3 * count // (2 * experts * 8)) * 8
    returned, pick, gate, prices = layer(
        assign.reshape(1, count),
        price.reshape(1, experts),
        router.T,
        tokens,
        w_in[0],
        w_out[0],
        lax.axis_size("dp"),
        capacity,
    )[:4]
    returned = returned.reshape(experts * capacity, width)
    picked = jnp.dot(pick, returned, preferred_element_type=jnp.float32)
    mixed = (gate.reshape(count)[:, None] * picked).astype(jnp.bfloat16)
    return (mixed, prices.reshape(experts))


def solution(mesh):
    return jax.shard_map(
        shards,
        mesh=mesh,
        in_specs=(
            P(("dp", "expert"), None),
            P(),
            P(),
            P("expert", None, "dp"),
            P("expert", "dp", None),
            P(("dp", "expert")),
        ),
        out_specs=(P(("dp", "expert"), None), P()),
        check_vma=False,
    )
```

```python
import functools

import jax
import jax.numpy as jnp
from jax import lax
from jax.experimental import pallas as pl
from jax.experimental.pallas import tpu as pltpu
from jax.sharding import PartitionSpec as P

BID_STEP = 0.01
EARLY = 4
MESH = pl.DeviceIdType.MESH
SCHED = (
    "s6", "s7", "s1", "s2", "a0", "a1", "w0", "w1", "a2", "b0", "s3", "a6",
    "a7", "s4", "c0", "f0", "g0", "w6", "a3", "s5", "w7", "p0", "b3", "w3",
    "a4", "c3", "f3", "w2", "a5", "g3", "b1", "c1", "w4", "p6", "p7", "p1",
    "f1", "w5", "g1", "h0", "r6", "b2", "c2", "r7", "f2", "p3", "g2", "p4",
    "r3", "p2", "r4", "p5", "r2", "r1", "r5", "r0",
)


def schedule(groups):
    if groups == 4:
        return SCHED
    order = [0] + list(range(groups - 1, 0, -1))
    steps = []
    for g in order[1:]:
        steps += [("s", 2 * g), ("s", 2 * g + 1)]
    steps += [("s", 1), ("a", 0), ("a", 1), ("w", 0), ("w", 1)]
    for i, g in enumerate(order):
        after = order[i + 1] if i + 1 < groups else None
        before = order[i - 1] if i else None
        steps += [("b", g)]
        if after is not None:
            steps += [("a", 2 * after)]
        steps += [("c", g), ("f", g)]
        if after is not None:
            steps += [("a", 2 * after + 1)]
        steps += [("g", g)]
        if after is not None:
            steps += [("w", 2 * after), ("w", 2 * after + 1)]
        steps += [("p", 2 * g), ("p", 2 * g + 1)]
        if before is not None:
            steps += [("r", 2 * before), ("r", 2 * before + 1)]
        if i == 1:
            steps += [("h", 0)]
    g = order[-1]
    steps += [("r", 2 * g), ("r", 2 * g + 1)]
    return [name + str(k) for name, k in steps]


def remote(src, dst, send, recv, a, b):
    return pltpu.make_async_remote_copy(
        src_ref=src, dst_ref=dst, send_sem=send, recv_sem=recv, device_id=(a, b), device_id_type=MESH
    )


def signal(dps, experts, a, b):
    barrier = pltpu.get_barrier_semaphore()
    for k in range(1, experts):
        pl.semaphore_signal(barrier, inc=1, device_id=(a, lax.rem(b + k, experts)), device_id_type=MESH)
    for k in range(1, dps):
        pl.semaphore_signal(barrier, inc=1, device_id=(lax.rem(a + k, dps), b), device_id_type=MESH)


def meet(dps, experts):
    pl.semaphore_wait(pltpu.get_barrier_semaphore(), experts + dps - 2)


def layer_kernel(
    dps, experts, capacity, spill, assign, price, router, tokens, w_in, w_out, back, pick, gate, prices, *refs
):
    if spill:
        rows, refs = refs[0], refs[1:]
        loaded, refs = refs[0], refs[1:]
    else:
        rows, refs = refs[0], refs[1:]
        loaded = None
    packed, best, bests, all_bests, win, wout, flat, hidden, part, pair, far, final, top = refs[:13]
    load_sem, own_sem, s1, r1, s2, r2, s3, r3, s4, r4, s5, r5, s6, r6, sb, rb, sd, rd = refs[13:]
    a, b = lax.axis_index("dp"), lax.axis_index("expert")
    nx, groups = dps // 2, experts // 2
    x, c = a // 2, lax.rem(a, 2)
    z, y = b // 2, lax.rem(b, 2)
    other = 2 * x + 1 - c
    count, width = tokens.shape
    ff = win.shape[1]
    cut = 512
    wide = 1024
    tall = 2 * dps * capacity
    half_width = width // 2
    load_in = pltpu.make_async_copy(w_in, win, load_sem.at[0])
    load_out = pltpu.make_async_copy(w_out, wout, load_sem.at[1])
    load_in.start()
    load_out.start()
    signal(dps, experts, a, b)

    order = list(range(groups))

    def behind(k):
        to = z
        for bit in range(groups.bit_length()):
            if order[k // 2] >> bit & 1:
                to = to + (1 - 2 * lax.rem(z // 2**bit, 2)) * 2**bit
        return 2 * to + lax.rem(y + k % 2, 2)

    ahead = behind

    def xrow(q):
        return 2 * lax.rem(x + q, nx) + c

    def xback(q):
        return 2 * lax.rem(x + nx - q, nx) + c

    def out(k):
        e = ahead(k)
        return remote(packed.at[k], rows.at[k, a], s1.at[k], r1.at[k], a, e)

    def out_best(k):
        return remote(best, bests.at[k], sb.at[k], rb.at[k], a, ahead(k))

    def spread_best(k):
        return remote(top, all_bests.at[k], sd.at[k], rd.at[k], lax.rem(a + k, dps), b)

    def fan(q, k):
        return remote(rows.at[k, a], rows.at[k, a], s2.at[q - 1, k], r2.at[q - 1, k], xrow(q), b)

    def fan_in(q, k):
        row = xback(q)
        return remote(rows.at[k, row], rows.at[k, row], s2.at[q - 1, k], r2.at[q - 1, k], row, b)

    def share(q, k):
        row = xback(q)
        return remote(rows.at[k, row], rows.at[k, row], s3.at[q, k], r3.at[q, k], other, b)

    def share_in(q, k):
        row = xback(q) + 1 - 2 * c
        return remote(rows.at[k, row], rows.at[k, row], s3.at[q, k], r3.at[q, k], other, b)

    def beside(q, k):
        return remote(
            part.at[k, xrow(q) + 1 - 2 * c], pair.at[q, k], s4.at[q, k], r4.at[q, k], other, b
        )

    def across(q, k, h):
        cols = pl.ds(h * half_width, half_width)
        return remote(
            pair.at[q, k, :, cols], far.at[q - 1, k, :, cols], s5.at[q - 1, k, h], r5.at[q - 1, k, h], xrow(q), b
        )

    def home(k, h):
        cols = pl.ds(h * half_width, half_width)
        return remote(final.at[k, :, cols], back.at[b, :, cols], s6.at[k, h], r6.at[k, h], a, behind(k))

    own = pltpu.make_async_copy(packed.at[0], rows.at[0, a], own_sem.at[0])
    own_back = pltpu.make_async_copy(final.at[0], back.at[b], own_sem.at[2])

    def arrive(k):
        if k == 0:
            own.wait()
        else:
            out(k).wait_recv()
        for q in range(1, nx):
            fan(q, k).start()
        share(0, k).start()

    def forward(k):
        for q in range(1, nx):
            fan_in(q, k).wait_recv()
            share(q, k).start()

    def first(t, carry):
        cols = pl.ds(pl.multiple_of(t * wide, wide), wide)
        raw = jnp.dot(flat[...], win[:, cols], preferred_element_type=jnp.float32)
        hidden[:, cols] = jax.nn.gelu(raw, approximate=True).astype(jnp.bfloat16)
        return carry

    def begin(g):
        for k in (2 * g, 2 * g + 1):
            for q in range(nx):
                share_in(q, k).wait_recv()
        if spill:
            load = pltpu.make_async_copy(rows.at[pl.ds(2 * g, 2)], loaded, own_sem.at[1])
            load.start()
            load.wait()

        def flatten(t, carry):
            cols = pl.ds(pl.multiple_of(t * cut, cut), cut)
            source = loaded[:, :, :, cols] if spill else rows[2 * g : 2 * g + 2, :, :, cols]
            block = source.astype(jnp.float32)
            flat[:, cols] = block.reshape(tall, cut).astype(jnp.bfloat16)
            return carry

        lax.fori_loop(0, width // cut, flatten, 0)
        if not waited:
            load_in.wait()
        lax.fori_loop(0, ff // wide // 2, first, 0)

    def middle(g):
        lax.fori_loop(ff // wide // 2, ff // wide, first, 0)
        if not waited:
            load_out.wait()
            waited.append(g)

    def finish(g, half):
        def second(t, carry):
            cols = pl.ds(pl.multiple_of(t * wide, wide), wide)
            res = jnp.dot(hidden[...], wout[:, cols], preferred_element_type=jnp.float32)
            part[2 * g : 2 * g + 2, :, :, cols] = res.reshape(2, dps, capacity, wide).astype(jnp.bfloat16)
            return carry

        steps = width // wide
        lax.fori_loop(half * steps // 2, (half + 1) * steps // 2, second, 0)
        if half == 1:
            for k in (2 * g, 2 * g + 1):
                for q in list(range(1, nx)) + [0]:
                    beside(q, k).start()

    def add_pair(k):
        for q in range(1, nx):
            beside(q, k).wait_recv()

        for h in range(2):
            for q in range(1, nx):

                def add(t, carry):
                    cols = pl.ds(pl.multiple_of(t * cut, cut), cut)
                    total = part[k, xrow(q), :, cols].astype(jnp.float32)
                    total = total + pair[q, k, :, cols].astype(jnp.float32)
                    pair[q, k, :, cols] = total.astype(jnp.bfloat16)
                    return carry

                lax.fori_loop(h * half_width // cut, (h + 1) * half_width // cut, add, 0)
                across(q, k, h).start()

    def add_far(k):
        beside(0, k).wait_recv()
        for h in range(2):
            for q in range(1, nx):
                across(q, k, h).wait_recv()

            def add(t, carry):
                cols = pl.ds(pl.multiple_of(t * cut, cut), cut)
                total = part[k, a, :, cols].astype(jnp.float32)
                total = total + pair[0, k, :, cols].astype(jnp.float32)
                for q in range(1, nx):
                    total = total + far[q - 1, k, :, cols].astype(jnp.float32)
                final[k, :, cols] = total.astype(jnp.bfloat16)
                return carry

            lax.fori_loop(h * half_width // cut, (h + 1) * half_width // cut, add, 0)
            if k:
                home(k, h).start()
        if k == 0:
            own_back.start()

    def highest_bid():
        for k in range(1, experts):
            out_best(k).wait_recv()
        highest = best[...]
        for k in range(1, experts):
            highest = jnp.maximum(highest, bests[k])
        top[...] = highest
        all_bests[0] = highest
        for k in range(1, dps):
            spread_best(k).start()

    waited = []
    named = assign[...]
    upper = lax.broadcasted_iota(jnp.int32, (count, count), 0)
    lower = lax.broadcasted_iota(jnp.int32, (count, count), 1)
    onehot = lax.broadcasted_iota(jnp.int32, (experts, count), 0) == named
    before = jnp.where(upper <= lower, 1.0, 0.0).astype(jnp.bfloat16)
    running = jnp.dot(
        jnp.where(onehot, 1.0, 0.0).astype(jnp.bfloat16), before, preferred_element_type=jnp.float32
    )
    slot = jnp.sum(jnp.where(onehot, running, 0.0), axis=0, keepdims=True).astype(jnp.int32) - 1
    place = named * capacity + slot

    def pack(low, high):
        lines = lax.broadcasted_iota(jnp.int32, (capacity, count), 0)
        chosen = jnp.concatenate(
            [jnp.where(place == ahead(k) * capacity + lines, 1.0, 0.0) for k in range(low, high)], axis=0
        ).astype(jnp.bfloat16)

        def some(t, carry):
            cols = pl.ds(pl.multiple_of(t * cut, cut), cut)
            block = jnp.dot(chosen, tokens[:, cols], preferred_element_type=jnp.float32)
            packed[low:high, :, cols] = block.reshape(high - low, capacity, cut).astype(jnp.bfloat16)
            return carry

        lax.fori_loop(0, width // cut, some, 0)

    def bids():
        affinity = lax.dot_general(
            router[...], tokens[...], (((1,), (1,)), ((), ())), preferred_element_type=jnp.float32
        )
        corner = lax.broadcasted_iota(jnp.int32, (experts, experts), 0) == lax.broadcasted_iota(
            jnp.int32, (experts, experts), 1
        )
        cost = jnp.sum(jnp.where(corner, price[...], 0.0), axis=1, keepdims=True)
        mine = jnp.sum(jnp.where(onehot, affinity, 0.0), axis=0, keepdims=True)
        rival = jnp.max(jnp.where(onehot, -1e30, affinity - cost), axis=0, keepdims=True)
        bid = mine - rival + BID_STEP
        high = jnp.max(jnp.where(onehot, bid, -1e30), axis=1, keepdims=True)
        best[...] = jnp.broadcast_to(high, best.shape)
        gate[...] = jax.nn.sigmoid(mine)
        diagonal = upper == lower
        spot = jnp.sum(jnp.where(diagonal, place.astype(jnp.float32), 0.0), axis=1, keepdims=True)
        slots = lax.broadcasted_iota(jnp.int32, (count, experts * capacity), 1)
        pick[...] = jnp.where(spot.astype(jnp.int32) == slots, 1.0, 0.0).astype(jnp.bfloat16)

    pack(0, experts)
    meet(dps, experts)
    own.start()
    early = [op for op in schedule(groups) if op[0] == "s"]
    for op in early[: EARLY]:
        out(int(op[1:])).start()
    bids()
    for k in range(1, experts):
        out_best(k).start()
    table = dict(s=lambda k: out(k).start(), a=arrive, w=forward, b=begin, c=middle, f=lambda g: finish(g, 0), g=lambda g: finish(g, 1), p=add_pair, r=add_far, h=lambda k: highest_bid())
    for op in schedule(groups):
        if op in early[:EARLY]:
            continue
        table[op[0]](int(op[1:]))
    own_back.wait()
    total = all_bests[0]
    for k in range(1, dps):
        spread_best(k).wait_recv()
        total = jnp.maximum(total, all_bests[k])
    square = (experts, experts)
    corner = lax.broadcasted_iota(jnp.int32, square, 0) == lax.broadcasted_iota(jnp.int32, square, 1)
    prices[...] = jnp.max(jnp.where(corner, total[:, :experts], -1e30), axis=0, keepdims=True)
    for k in range(1, dps):
        spread_best(k).wait_send()
    for k in range(1, experts):
        e = ahead(k)
        for h in range(2):
            cols = pl.ds(h * half_width, half_width)
            remote(final.at[k, :, cols], back.at[e, :, cols], s6.at[k, h], r6.at[k, h], a, e).wait_recv()
            home(k, h).wait_send()
        out(k).wait_send()
        out_best(k).wait_send()
    for k in range(experts):
        for q in range(1, nx):
            fan(q, k).wait_send()
            for h in range(2):
                across(q, k, h).wait_send()
        for q in range(nx):
            share(q, k).wait_send()
            beside(q, k).wait_send()


def layer(assign, price, router, tokens, w_in, w_out, dps, capacity):
    experts = router.shape[0]
    count, width = tokens.shape
    nx = dps // 2
    ff = w_in.shape[1]
    tall = 2 * dps * capacity
    dtype = tokens.dtype
    sem = pltpu.SemaphoreType.DMA
    anywhere = pl.BlockSpec(memory_space=pl.ANY)
    inside = pl.BlockSpec(memory_space=pltpu.VMEM)
    landing = (experts, dps, capacity, width)
    note = (experts, 128)
    spill = experts * dps * capacity * width > 4 * 1024 * 1024
    outs = [
        jax.ShapeDtypeStruct((experts, capacity, width), dtype),
        jax.ShapeDtypeStruct((count, experts * capacity), jnp.bfloat16),
        jax.ShapeDtypeStruct((1, count), jnp.float32),
        jax.ShapeDtypeStruct((1, experts), jnp.float32),
    ]
    places = [anywhere, inside, inside, inside]
    if spill:
        outs.append(jax.ShapeDtypeStruct(landing, dtype))
        places.append(anywhere)
        held = [pltpu.VMEM((2, dps, capacity, width), dtype)]
    else:
        held = [pltpu.VMEM(landing, dtype)]
    return pl.pallas_call(
        functools.partial(layer_kernel, dps, experts, capacity, spill),
        out_shape=tuple(outs),
        in_specs=[inside, inside, inside, inside, anywhere, anywhere],
        out_specs=tuple(places),
        scratch_shapes=held + [
            pltpu.VMEM((experts, capacity, width), dtype),
            pltpu.VMEM(note, jnp.float32),
            pltpu.VMEM((experts,) + note, jnp.float32),
            pltpu.VMEM((dps,) + note, jnp.float32),
            pltpu.VMEM((width, ff), dtype),
            pltpu.VMEM((ff, width), dtype),
            pltpu.VMEM((tall, width), dtype),
            pltpu.VMEM((tall, ff), dtype),
            pltpu.VMEM((experts, dps, capacity, width), dtype),
            pltpu.VMEM((nx, experts, capacity, width), dtype),
            pltpu.VMEM((nx - 1, experts, capacity, width), dtype),
            pltpu.VMEM((experts, capacity, width), dtype),
            pltpu.VMEM(note, jnp.float32),
            sem((2,)),
            sem((3,)),
            sem((experts,)),
            sem((experts,)),
            sem((nx - 1, experts)),
            sem((nx - 1, experts)),
            sem((nx, experts)),
            sem((nx, experts)),
            sem((nx, experts)),
            sem((nx, experts)),
            sem((nx - 1, experts, 2)),
            sem((nx - 1, experts, 2)),
            sem((experts, 2)),
            sem((experts, 2)),
            sem((experts,)),
            sem((experts,)),
            sem((dps,)),
            sem((dps,)),
        ],
        compiler_params=pltpu.CompilerParams(
            collective_id=0, has_side_effects=True, vmem_limit_bytes=63 * 1024 * 1024
        ),
        name="layer",
    )(assign, price, router, tokens, w_in, w_out)


def shards(tokens, router, price, w_in, w_out, assign):
    experts = router.shape[1]
    count, width = tokens.shape
    capacity = -(-3 * count // (2 * experts * 8)) * 8
    returned, pick, gate, prices = layer(
        assign.reshape(1, count),
        price.reshape(1, experts),
        router.T,
        tokens,
        w_in[0],
        w_out[0],
        lax.axis_size("dp"),
        capacity,
    )[:4]
    returned = returned.reshape(experts * capacity, width)
    picked = jnp.dot(pick, returned, preferred_element_type=jnp.float32)
    mixed = (gate.reshape(count)[:, None] * picked).astype(jnp.bfloat16)
    return (mixed, prices.reshape(experts))


def solution(mesh):
    return jax.shard_map(
        shards,
        mesh=mesh,
        in_specs=(
            P(("dp", "expert"), None),
            P(),
            P(),
            P("expert", None, "dp"),
            P("expert", "dp", None),
            P(("dp", "expert")),
        ),
        out_specs=(P(("dp", "expert"), None), P()),
        check_vma=False,
    )
```

```python
import functools

import jax
import jax.numpy as jnp
from jax import lax
from jax.experimental import pallas as pl
from jax.experimental.pallas import tpu as pltpu
from jax.sharding import PartitionSpec as P

BID_STEP = 0.01
EARLY = 3
MESH = pl.DeviceIdType.MESH
SCHED = (
    "s6", "s7", "s1", "a1", "s2", "a0", "a2", "s3", "a6", "s4", "s5", "w0",
    "w1", "b0", "c0", "a7", "f0", "w6", "w7", "g0", "a3", "b3", "c3", "a5",
    "w2", "f3", "g3", "a4", "w3", "p7", "b1", "c1", "p6", "p1", "f1", "w4",
    "w5", "r7", "g1", "b2", "c2", "p3", "r6", "f2", "h0", "g2", "p5", "p4",
    "r3", "r5", "p2", "r4", "p0", "r2", "r1", "r0",
)


def schedule(groups):
    if groups == 4:
        return SCHED
    order = [0] + list(range(groups - 1, 0, -1))
    steps = []
    for g in order[1:]:
        steps += [("s", 2 * g), ("s", 2 * g + 1)]
    steps += [("s", 1), ("a", 0), ("a", 1), ("w", 0), ("w", 1)]
    for i, g in enumerate(order):
        after = order[i + 1] if i + 1 < groups else None
        before = order[i - 1] if i else None
        steps += [("b", g)]
        if after is not None:
            steps += [("a", 2 * after)]
        steps += [("c", g), ("f", g)]
        if after is not None:
            steps += [("a", 2 * after + 1)]
        steps += [("g", g)]
        if after is not None:
            steps += [("w", 2 * after), ("w", 2 * after + 1)]
        steps += [("p", 2 * g), ("p", 2 * g + 1)]
        if before is not None:
            steps += [("r", 2 * before), ("r", 2 * before + 1)]
        if i == 1:
            steps += [("h", 0)]
    g = order[-1]
    steps += [("r", 2 * g), ("r", 2 * g + 1)]
    return [name + str(k) for name, k in steps]


def remote(src, dst, send, recv, a, b):
    return pltpu.make_async_remote_copy(
        src_ref=src, dst_ref=dst, send_sem=send, recv_sem=recv, device_id=(a, b), device_id_type=MESH
    )


def signal(dps, experts, a, b):
    barrier = pltpu.get_barrier_semaphore()
    for k in range(1, experts):
        pl.semaphore_signal(barrier, inc=1, device_id=(a, lax.rem(b + k, experts)), device_id_type=MESH)
    for k in range(1, dps):
        pl.semaphore_signal(barrier, inc=1, device_id=(lax.rem(a + k, dps), b), device_id_type=MESH)


def meet(dps, experts):
    pl.semaphore_wait(pltpu.get_barrier_semaphore(), experts + dps - 2)


def layer_kernel(
    dps, experts, capacity, spill, assign, price, router, tokens, w_in, w_out, back, pick, gate, prices, *refs
):
    if spill:
        rows, refs = refs[0], refs[1:]
        loaded, refs = refs[0], refs[1:]
    else:
        rows, refs = refs[0], refs[1:]
        loaded = None
    packed, best, bests, all_bests, win, wout, flat, hidden, part, pair, far, final, top = refs[:13]
    load_sem, own_sem, s1, r1, s2, r2, s3, r3, s4, r4, s5, r5, s6, r6, sb, rb, sd, rd = refs[13:]
    a, b = lax.axis_index("dp"), lax.axis_index("expert")
    nx, groups = dps // 2, experts // 2
    x, c = a // 2, lax.rem(a, 2)
    z, y = b // 2, lax.rem(b, 2)
    other = 2 * x + 1 - c
    count, width = tokens.shape
    ff = win.shape[1]
    cut = 512
    wide = 1024
    tall = 2 * dps * capacity
    half_width = width // 2
    load_in = pltpu.make_async_copy(w_in, win, load_sem.at[0])
    load_out = pltpu.make_async_copy(w_out, wout, load_sem.at[1])
    load_in.start()
    load_out.start()
    signal(dps, experts, a, b)

    order = list(range(groups))

    def behind(k):
        to = z
        for bit in range(groups.bit_length()):
            if order[k // 2] >> bit & 1:
                to = to + (1 - 2 * lax.rem(z // 2**bit, 2)) * 2**bit
        return 2 * to + lax.rem(y + k % 2, 2)

    ahead = behind

    def xrow(q):
        return 2 * lax.rem(x + q, nx) + c

    def xback(q):
        return 2 * lax.rem(x + nx - q, nx) + c

    def out(k):
        e = ahead(k)
        return remote(packed.at[k], rows.at[k, a], s1.at[k], r1.at[k], a, e)

    def out_best(k):
        return remote(best, bests.at[k], sb.at[k], rb.at[k], a, ahead(k))

    def spread_best(k):
        return remote(top, all_bests.at[k], sd.at[k], rd.at[k], lax.rem(a + k, dps), b)

    def fan(q, k):
        return remote(rows.at[k, a], rows.at[k, a], s2.at[q - 1, k], r2.at[q - 1, k], xrow(q), b)

    def fan_in(q, k):
        row = xback(q)
        return remote(rows.at[k, row], rows.at[k, row], s2.at[q - 1, k], r2.at[q - 1, k], row, b)

    def share(q, k):
        row = xback(q)
        return remote(rows.at[k, row], rows.at[k, row], s3.at[q, k], r3.at[q, k], other, b)

    def share_in(q, k):
        row = xback(q) + 1 - 2 * c
        return remote(rows.at[k, row], rows.at[k, row], s3.at[q, k], r3.at[q, k], other, b)

    def beside(q, k):
        return remote(
            part.at[k, xrow(q) + 1 - 2 * c], pair.at[q, k], s4.at[q, k], r4.at[q, k], other, b
        )

    def across(q, k, h):
        cols = pl.ds(h * half_width, half_width)
        return remote(
            pair.at[q, k, :, cols], far.at[q - 1, k, :, cols], s5.at[q - 1, k, h], r5.at[q - 1, k, h], xrow(q), b
        )

    def home(k, h):
        cols = pl.ds(h * half_width, half_width)
        return remote(final.at[k, :, cols], back.at[b, :, cols], s6.at[k, h], r6.at[k, h], a, behind(k))

    own = pltpu.make_async_copy(packed.at[0], rows.at[0, a], own_sem.at[0])
    own_back = pltpu.make_async_copy(final.at[0], back.at[b], own_sem.at[2])

    def arrive(k):
        if k == 0:
            own.wait()
        else:
            out(k).wait_recv()
        for q in range(1, nx):
            fan(q, k).start()
        share(0, k).start()

    def forward(k):
        for q in range(1, nx):
            fan_in(q, k).wait_recv()
            share(q, k).start()

    def first(t, carry):
        cols = pl.ds(pl.multiple_of(t * wide, wide), wide)
        raw = jnp.dot(flat[...], win[:, cols], preferred_element_type=jnp.float32)
        hidden[:, cols] = jax.nn.gelu(raw, approximate=True).astype(jnp.bfloat16)
        return carry

    def begin(g):
        for k in (2 * g, 2 * g + 1):
            for q in range(nx):
                share_in(q, k).wait_recv()
        if spill:
            load = pltpu.make_async_copy(rows.at[pl.ds(2 * g, 2)], loaded, own_sem.at[1])
            load.start()
            load.wait()

        def flatten(t, carry):
            cols = pl.ds(pl.multiple_of(t * cut, cut), cut)
            source = loaded[:, :, :, cols] if spill else rows[2 * g : 2 * g + 2, :, :, cols]
            block = source.astype(jnp.float32)
            flat[:, cols] = block.reshape(tall, cut).astype(jnp.bfloat16)
            return carry

        lax.fori_loop(0, width // cut, flatten, 0)
        if not waited:
            load_in.wait()
        lax.fori_loop(0, ff // wide // 2, first, 0)

    def middle(g):
        lax.fori_loop(ff // wide // 2, ff // wide, first, 0)
        if not waited:
            load_out.wait()
            waited.append(g)

    def finish(g, half):
        def second(t, carry):
            cols = pl.ds(pl.multiple_of(t * wide, wide), wide)
            res = jnp.dot(hidden[...], wout[:, cols], preferred_element_type=jnp.float32)
            part[2 * g : 2 * g + 2, :, :, cols] = res.reshape(2, dps, capacity, wide).astype(jnp.bfloat16)
            return carry

        steps = width // wide
        lax.fori_loop(half * steps // 2, (half + 1) * steps // 2, second, 0)
        if half == 1:
            for k in (2 * g, 2 * g + 1):
                for q in list(range(1, nx)) + [0]:
                    beside(q, k).start()

    def add_pair(k):
        for q in range(1, nx):
            beside(q, k).wait_recv()

        for h in range(2):
            for q in range(1, nx):

                def add(t, carry):
                    cols = pl.ds(pl.multiple_of(t * cut, cut), cut)
                    total = part[k, xrow(q), :, cols].astype(jnp.float32)
                    total = total + pair[q, k, :, cols].astype(jnp.float32)
                    pair[q, k, :, cols] = total.astype(jnp.bfloat16)
                    return carry

                lax.fori_loop(h * half_width // cut, (h + 1) * half_width // cut, add, 0)
                across(q, k, h).start()

    def add_far(k):
        beside(0, k).wait_recv()
        for h in range(2):
            for q in range(1, nx):
                across(q, k, h).wait_recv()

            def add(t, carry):
                cols = pl.ds(pl.multiple_of(t * cut, cut), cut)
                total = part[k, a, :, cols].astype(jnp.float32)
                total = total + pair[0, k, :, cols].astype(jnp.float32)
                for q in range(1, nx):
                    total = total + far[q - 1, k, :, cols].astype(jnp.float32)
                final[k, :, cols] = total.astype(jnp.bfloat16)
                return carry

            lax.fori_loop(h * half_width // cut, (h + 1) * half_width // cut, add, 0)
            if k:
                home(k, h).start()
        if k == 0:
            own_back.start()

    def highest_bid():
        for k in range(1, experts):
            out_best(k).wait_recv()
        highest = best[...]
        for k in range(1, experts):
            highest = jnp.maximum(highest, bests[k])
        top[...] = highest
        all_bests[0] = highest
        for k in range(1, dps):
            spread_best(k).start()

    waited = []
    named = assign[...]
    upper = lax.broadcasted_iota(jnp.int32, (count, count), 0)
    lower = lax.broadcasted_iota(jnp.int32, (count, count), 1)
    onehot = lax.broadcasted_iota(jnp.int32, (experts, count), 0) == named
    before = jnp.where(upper <= lower, 1.0, 0.0).astype(jnp.bfloat16)
    running = jnp.dot(
        jnp.where(onehot, 1.0, 0.0).astype(jnp.bfloat16), before, preferred_element_type=jnp.float32
    )
    slot = jnp.sum(jnp.where(onehot, running, 0.0), axis=0, keepdims=True).astype(jnp.int32) - 1
    place = named * capacity + slot

    def pack(low, high):
        lines = lax.broadcasted_iota(jnp.int32, (capacity, count), 0)
        chosen = jnp.concatenate(
            [jnp.where(place == ahead(k) * capacity + lines, 1.0, 0.0) for k in range(low, high)], axis=0
        ).astype(jnp.bfloat16)

        def some(t, carry):
            cols = pl.ds(pl.multiple_of(t * cut, cut), cut)
            block = jnp.dot(chosen, tokens[:, cols], preferred_element_type=jnp.float32)
            packed[low:high, :, cols] = block.reshape(high - low, capacity, cut).astype(jnp.bfloat16)
            return carry

        lax.fori_loop(0, width // cut, some, 0)

    def bids():
        affinity = lax.dot_general(
            router[...], tokens[...], (((1,), (1,)), ((), ())), preferred_element_type=jnp.float32
        )
        corner = lax.broadcasted_iota(jnp.int32, (experts, experts), 0) == lax.broadcasted_iota(
            jnp.int32, (experts, experts), 1
        )
        cost = jnp.sum(jnp.where(corner, price[...], 0.0), axis=1, keepdims=True)
        mine = jnp.sum(jnp.where(onehot, affinity, 0.0), axis=0, keepdims=True)
        rival = jnp.max(jnp.where(onehot, -1e30, affinity - cost), axis=0, keepdims=True)
        bid = mine - rival + BID_STEP
        high = jnp.max(jnp.where(onehot, bid, -1e30), axis=1, keepdims=True)
        best[...] = jnp.broadcast_to(high, best.shape)
        gate[...] = jax.nn.sigmoid(mine)
        diagonal = upper == lower
        spot = jnp.sum(jnp.where(diagonal, place.astype(jnp.float32), 0.0), axis=1, keepdims=True)
        slots = lax.broadcasted_iota(jnp.int32, (count, experts * capacity), 1)
        pick[...] = jnp.where(spot.astype(jnp.int32) == slots, 1.0, 0.0).astype(jnp.bfloat16)

    pack(0, experts)
    meet(dps, experts)
    own.start()
    early = [op for op in schedule(groups) if op[0] == "s"]
    for op in early[: EARLY]:
        out(int(op[1:])).start()
    bids()
    for k in range(1, experts):
        out_best(k).start()
    table = dict(s=lambda k: out(k).start(), a=arrive, w=forward, b=begin, c=middle, f=lambda g: finish(g, 0), g=lambda g: finish(g, 1), p=add_pair, r=add_far, h=lambda k: highest_bid())
    for op in schedule(groups):
        if op in early[:EARLY]:
            continue
        table[op[0]](int(op[1:]))
    own_back.wait()
    total = all_bests[0]
    for k in range(1, dps):
        spread_best(k).wait_recv()
        total = jnp.maximum(total, all_bests[k])
    square = (experts, experts)
    corner = lax.broadcasted_iota(jnp.int32, square, 0) == lax.broadcasted_iota(jnp.int32, square, 1)
    prices[...] = jnp.max(jnp.where(corner, total[:, :experts], -1e30), axis=0, keepdims=True)
    for k in range(1, dps):
        spread_best(k).wait_send()
    for k in range(1, experts):
        e = ahead(k)
        for h in range(2):
            cols = pl.ds(h * half_width, half_width)
            remote(final.at[k, :, cols], back.at[e, :, cols], s6.at[k, h], r6.at[k, h], a, e).wait_recv()
            home(k, h).wait_send()
        out(k).wait_send()
        out_best(k).wait_send()
    for k in range(experts):
        for q in range(1, nx):
            fan(q, k).wait_send()
            for h in range(2):
                across(q, k, h).wait_send()
        for q in range(nx):
            share(q, k).wait_send()
            beside(q, k).wait_send()


def layer(assign, price, router, tokens, w_in, w_out, dps, capacity):
    experts = router.shape[0]
    count, width = tokens.shape
    nx = dps // 2
    ff = w_in.shape[1]
    tall = 2 * dps * capacity
    dtype = tokens.dtype
    sem = pltpu.SemaphoreType.DMA
    anywhere = pl.BlockSpec(memory_space=pl.ANY)
    inside = pl.BlockSpec(memory_space=pltpu.VMEM)
    landing = (experts, dps, capacity, width)
    note = (experts, 128)
    spill = experts * dps * capacity * width > 4 * 1024 * 1024
    outs = [
        jax.ShapeDtypeStruct((experts, capacity, width), dtype),
        jax.ShapeDtypeStruct((count, experts * capacity), jnp.bfloat16),
        jax.ShapeDtypeStruct((1, count), jnp.float32),
        jax.ShapeDtypeStruct((1, experts), jnp.float32),
    ]
    places = [anywhere, inside, inside, inside]
    if spill:
        outs.append(jax.ShapeDtypeStruct(landing, dtype))
        places.append(anywhere)
        held = [pltpu.VMEM((2, dps, capacity, width), dtype)]
    else:
        held = [pltpu.VMEM(landing, dtype)]
    return pl.pallas_call(
        functools.partial(layer_kernel, dps, experts, capacity, spill),
        out_shape=tuple(outs),
        in_specs=[inside, inside, inside, inside, anywhere, anywhere],
        out_specs=tuple(places),
        scratch_shapes=held + [
            pltpu.VMEM((experts, capacity, width), dtype),
            pltpu.VMEM(note, jnp.float32),
            pltpu.VMEM((experts,) + note, jnp.float32),
            pltpu.VMEM((dps,) + note, jnp.float32),
            pltpu.VMEM((width, ff), dtype),
            pltpu.VMEM((ff, width), dtype),
            pltpu.VMEM((tall, width), dtype),
            pltpu.VMEM((tall, ff), dtype),
            pltpu.VMEM((experts, dps, capacity, width), dtype),
            pltpu.VMEM((nx, experts, capacity, width), dtype),
            pltpu.VMEM((nx - 1, experts, capacity, width), dtype),
            pltpu.VMEM((experts, capacity, width), dtype),
            pltpu.VMEM(note, jnp.float32),
            sem((2,)),
            sem((3,)),
            sem((experts,)),
            sem((experts,)),
            sem((nx - 1, experts)),
            sem((nx - 1, experts)),
            sem((nx, experts)),
            sem((nx, experts)),
            sem((nx, experts)),
            sem((nx, experts)),
            sem((nx - 1, experts, 2)),
            sem((nx - 1, experts, 2)),
            sem((experts, 2)),
            sem((experts, 2)),
            sem((experts,)),
            sem((experts,)),
            sem((dps,)),
            sem((dps,)),
        ],
        compiler_params=pltpu.CompilerParams(
            collective_id=0, has_side_effects=True, vmem_limit_bytes=63 * 1024 * 1024
        ),
        name="layer",
    )(assign, price, router, tokens, w_in, w_out)


def shards(tokens, router, price, w_in, w_out, assign):
    experts = router.shape[1]
    count, width = tokens.shape
    capacity = -(-3 * count // (2 * experts * 8)) * 8
    returned, pick, gate, prices = layer(
        assign.reshape(1, count),
        price.reshape(1, experts),
        router.T,
        tokens,
        w_in[0],
        w_out[0],
        lax.axis_size("dp"),
        capacity,
    )[:4]
    returned = returned.reshape(experts * capacity, width)
    picked = jnp.dot(pick, returned, preferred_element_type=jnp.float32)
    mixed = (gate.reshape(count)[:, None] * picked).astype(jnp.bfloat16)
    return (mixed, prices.reshape(experts))


def solution(mesh):
    return jax.shard_map(
        shards,
        mesh=mesh,
        in_specs=(
            P(("dp", "expert"), None),
            P(),
            P(),
            P("expert", None, "dp"),
            P("expert", "dp", None),
            P(("dp", "expert")),
        ),
        out_specs=(P(("dp", "expert"), None), P()),
        check_vma=False,
    )
```
